32 devices in a mesh: groups: 2 (over x), seq: 16 (over z, y, core).
Axes of the slice: x: 2, y: 2, z: 4, core: 2. Of those that a mesh axis runs over, the one named last changes fastest.
Arguments:
- tokens: bfloat16 [32768, 1024], P(('groups', 'seq')), parts along dimension 0, may hold values from -6 to 6
- doc_start: int32 [32768], P(('groups', 'seq')), parts along dimension 0, may hold values from 0 to 1
- level_index: int32 [32768], P(('groups', 'seq')), parts along dimension 0, may hold values from 0 to 63
- level_table: float32 [64, 18], replicated, may hold values from 0.0004 to 4.1, as said below
- conv_weight: float32 [4, 1024], replicated, may hold values from -3 to 3
- query_weight: bfloat16 [1024, 1024], replicated, may hold values from -0.1875 to 0.1875
- key_weight: bfloat16 [1024, 1024], replicated, may hold values from -0.1875 to 0.1875
- value_weight: bfloat16 [1024, 1024], replicated, may hold values from -0.1875 to 0.1875
- norm_gain: float32 [1024], replicated, may hold values from 0.5 to 1.5
Outputs:
- mixed: bfloat16 [32768, 1024], P(('groups', 'seq')), parts along dimension 0
The draws below stay inside these ranges and needn't reach their ends.
There are 2 independent parts, one for each index of `groups`. The reference program is written for one: setup_inputs(seed, part) draws one part's arguments, and reference() takes and returns one part's arrays. A program takes and returns all parts, laid end to end along the dimension named above; an argument that names none is the same for every part. Nothing has to cross between parts.
Inputs may be any that keep to these rules, and one draw needn't show every extreme that they name: `level_table`: positive entries.
All inputs are finite; a program needn't handle non-finite values.
Results may differ from the reference program's by a relative error of at most 0.007.
Values may be sent and summed in bfloat16 or wider, within the bound.
No kernel may reach another device: no remote copies, remote signals or barrier semaphores. Data moves between devices by JAX's collectives and lax.ppermute only.
A program may use at most 128 MiB of HBM per device.

```python
import jax
import jax.numpy as jnp
from jax import lax

D = 1024
HEADS = 8
HEAD_DIM = 128
CONV = 4
LEVELS = 18
TABLE = 64
TOK_DEV = 1024
TOKENS = 16384
N_SEQ = 16


def draw_doc_start(key, part):
    draw_rate = max(TOK_DEV // 2, 1)
    picked = jax.random.randint(jax.random.fold_in(key, 11), (TOKENS,), 0, draw_rate)
    position = jnp.arange(TOKENS, dtype=jnp.int32)
    inside = (position >= TOKENS // 8) & (position < TOKENS * 3 // 8)
    return ((picked == 0) & inside).astype(jnp.int32)


def draw_level_table(key, part):
    level_ids = jnp.arange(LEVELS, dtype=jnp.float32)
    spread = jax.random.uniform(jax.random.fold_in(key, 5), (TABLE, LEVELS), jnp.float32, -0.7, 0.7)
    return jnp.exp(spread) * jnp.exp2(-0.5 * level_ids)[None, :]


def plant(values, rng, low, top_value):
    place = [jax.random.randint(jax.random.fold_in(rng, axis), (), 0, length) for axis, length in enumerate(values.shape)]
    longest = values.shape.index(max(values.shape))
    beside = place[:longest] + [(place[longest] + 1) % values.shape[longest]] + place[longest + 1:]
    return values.at[tuple(place)].set(low).at[tuple(beside)].set(top_value)


def shard_levels(rng, extent, cuts, smallest, largest):
    factor_of = 1.0
    for dim, parts in cuts:
        draws = jax.random.uniform(jax.random.fold_in(jax.random.fold_in(rng, 6), dim), (parts,), jnp.float32, smallest / len(cuts), largest / len(cuts))
        factor_of = factor_of * jnp.repeat(jnp.exp(draws), extent[dim] // parts).reshape((-1,) + (1,) * (len(extent) - 1 - dim))
    return factor_of


def bell_draw(stream_key, extent, deviation, reach, split=(), held_as=jnp.bfloat16):
    gain = shard_levels(stream_key, extent, split, -0.22, 0.18) if split else 1.0
    values = jax.random.normal(stream_key, extent, jnp.float32) * deviation * gain
    return jnp.minimum(jnp.maximum(values, -reach), reach).astype(held_as)


def setup_inputs(seed: int = 0, part: int = 0) -> dict:
    key_of = jax.random.split(jax.random.key(seed), 10)
    part_splits = jax.random.split(jax.random.fold_in(key_of[9], part), 10)
    return {
        "tokens": bell_draw(part_splits[0], (TOKENS, D), 1.0, 6.0, ((0, 16),)),
        "doc_start": draw_doc_start(jax.random.fold_in(jax.random.fold_in(key_of[9], part), 71), part),
        "level_index": plant(jax.random.randint(part_splits[2], (TOKENS,), 0, TABLE), jax.random.fold_in(part_splits[2], 1), 0, TABLE - 1).astype(jnp.int32),
        "level_table": draw_level_table(jax.random.fold_in(key_of[9], 71), part),
        "conv_weight": bell_draw(key_of[4], (CONV, D), 0.5, 3.0, (), jnp.float32),
        "query_weight": bell_draw(key_of[5], (D, D), D ** -0.5, 0.1875),
        "key_weight": bell_draw(key_of[6], (D, D), D ** -0.5, 0.1875),
        "value_weight": bell_draw(key_of[7], (D, D), D ** -0.5, 0.1875),
        "norm_gain": jnp.clip(1.0 + 0.1 * jax.random.normal(key_of[8], (D,), jnp.float32), 0.5, 1.5),
    }


highest = lax.Precision.HIGHEST
epsilon = 1e-05

def bit_count(values, bit_width):
    counted = jnp.zeros_like(values)
    for bit_index in range(bit_width):
        counted = counted + (values >= 1 << bit_index).astype(jnp.int32)
    return counted

def reference(tokens, doc_start, level_index, level_table, conv_weight, query_weight, key_weight, value_weight, norm_gain):
    tap_count = conv_weight.shape[0]
    doc_id = jnp.cumsum(doc_start).astype(jnp.int32)
    padded = jnp.concatenate([jnp.zeros((tap_count - 1, D), tokens.dtype), tokens], 0)
    doc_pad = jnp.concatenate([jnp.full((tap_count - 1,), -1, jnp.int32), doc_id], 0)
    conv_sum = jnp.zeros((TOKENS, D), jnp.float32)
    for tap_index in range(tap_count):
        low_row = tap_count - 1 - tap_index
        shifted = padded[low_row:low_row + TOKENS].astype(jnp.float32)
        same_doc = (doc_pad[low_row:low_row + TOKENS] == doc_id).astype(jnp.float32)
        conv_sum = conv_sum + conv_weight[tap_index][None, :] * shifted * same_doc[:, None]
    conv_out = conv_sum.astype(jnp.bfloat16)
    queries = jnp.dot(conv_out, query_weight, preferred_element_type=jnp.float32).astype(jnp.bfloat16)
    key_rows = jnp.dot(conv_out, key_weight, preferred_element_type=jnp.float32).astype(jnp.bfloat16)
    values = jnp.dot(conv_out, value_weight, preferred_element_type=jnp.float32).astype(jnp.bfloat16)
    level_weight = level_table[level_index]
    block_count = N_SEQ
    local_bits = TOK_DEV.bit_length() - 1
    chain_bits = N_SEQ.bit_length() - 1
    query_blocks = queries.reshape(block_count, TOK_DEV, HEADS, HEAD_DIM)
    key_blocks = key_rows.reshape(block_count, TOK_DEV, HEADS, HEAD_DIM)
    value_blocks = values.reshape(block_count, TOK_DEV, HEADS, HEAD_DIM)
    doc_blocks = doc_id.reshape(block_count, TOK_DEV)
    weight_blocks = level_weight.reshape(block_count, TOK_DEV, LEVELS)
    last_doc = doc_blocks[:, TOK_DEV - 1]
    tail_mask = (doc_blocks == last_doc[:, None]).astype(jnp.float32)
    key_tail = key_blocks.astype(jnp.float32) * tail_mask[:, :, None, None]
    states = jnp.einsum('bnhd,bnhe->bhde', key_tail, value_blocks.astype(jnp.float32), precision=highest)
    positions = jnp.arange(TOK_DEV, dtype=jnp.int32)
    level_local = bit_count(jnp.bitwise_xor(positions[:, None], positions[None, :]), local_bits)
    causal = positions[:, None] >= positions[None, :]
    blocks = jnp.arange(block_count, dtype=jnp.int32)
    gain_heads = norm_gain.reshape(HEADS, HEAD_DIM)

    def one_block(inputs):
        block_index, query_here, key_here, value_here, doc_here, weight_here = inputs
        same_doc = (doc_here[:, None] == doc_here[None, :]) & causal
        weight = jnp.zeros((TOK_DEV, TOK_DEV), jnp.float32)
        for level_id in range(local_bits + 1):
            weight = weight + jnp.where(level_local == level_id, weight_here[:, level_id:level_id + 1], 0.0)
        weight = jnp.where(same_doc, weight, 0.0)
        scores = jnp.einsum('thd,shd->hts', query_here.astype(jnp.float32), key_here.astype(jnp.float32))
        weighted = (scores * weight[None]).astype(jnp.bfloat16)
        near_sum = jnp.einsum('hts,shd->thd', weighted.astype(jnp.float32), value_here.astype(jnp.float32))
        first_doc = doc_here[0]
        earlier = (last_doc == first_doc) & (blocks < block_index)
        token_gate = (doc_here == first_doc).astype(jnp.float32)
        level_far = bit_count(jnp.bitwise_xor(blocks, block_index), chain_bits) - 1
        query_wide = query_here.astype(jnp.float32)
        combined = near_sum
        for bit_index in range(chain_bits):
            selector = (earlier & (level_far == bit_index)).astype(jnp.float32)
            level_state = jnp.einsum('b,bhde->hde', selector, states, precision=highest)
            product = jnp.einsum('thd,hde->the', query_wide, level_state, precision=highest)
            scale_now = weight_here[:, local_bits + 1 + bit_index] * token_gate
            combined = combined + scale_now[:, None, None] * product
        inv_norm = lax.rsqrt(lax.optimization_barrier(jnp.mean(combined * combined, axis=-1, keepdims=True)) + epsilon)
        return (combined * inv_norm * gain_heads[None]).reshape(TOK_DEV, D).astype(jnp.bfloat16)
    results = lax.map(one_block, (blocks, query_blocks, key_blocks, value_blocks, doc_blocks, weight_blocks))
    return results.reshape(TOKENS, D)
```

```python
import functools

import jax
import jax.numpy as jnp
from jax import lax
from jax.experimental import pallas as pl
from jax.experimental.pallas import tpu as pltpu
from jax.sharding import PartitionSpec as P

HEADS = 8
HEAD_DIM = 128
CHUNK = 256
FLAG_ROWS = 16
DOC_COL = 32
highest = lax.Precision.HIGHEST
epsilon = 1e-05
F32 = jnp.float32
BF16 = jnp.bfloat16


def dot(a, b, dims=((1,), (0,)), precision=None):
    return lax.dot_general(a, b, (dims, ((), ())), precision=precision, preferred_element_type=F32)


def state_kernel(
    x_ref, halo_ref, ds_ref, idx_ref, table_ref, cw_ref, wk_hbm, wv_hbm,
    conv_ref, k_ref, v_ref, aux_ref, pay_ref, loc_ref,
    wk_ref, wv_ref, xs, feat, coef, st, sems,
):
    rows, width = x_ref.shape
    chunks = rows // CHUNK
    taps = cw_ref.shape[0]
    table_rows, levels = table_ref.shape
    half = HEADS // 2 * HEAD_DIM
    copy_k = pltpu.make_async_copy(wk_hbm, wk_ref, sems.at[0])
    copy_v = pltpu.make_async_copy(wv_hbm, wv_ref, sems.at[1])
    copy_k.start()
    copy_v.start()

    xs[0:8, :] = halo_ref[...].astype(F32)
    for c in range(chunks):
        xs[8 + c * CHUNK : 8 + (c + 1) * CHUNK, :] = x_ref[c * CHUNK : (c + 1) * CHUNK, :].astype(F32)

    starts = ds_ref[...].astype(F32)
    upper = (
        lax.broadcasted_iota(jnp.int32, (CHUNK, CHUNK), 0)
        <= lax.broadcasted_iota(jnp.int32, (CHUNK, CHUNK), 1)
    ).astype(BF16)
    starts8 = jnp.broadcast_to(starts, (8, rows))
    lane = lax.broadcasted_iota(jnp.int32, (8, rows), 1)
    base = jnp.zeros((8, 1), F32)
    docs = []
    for c in range(chunks):
        part = dot(starts8[:, c * CHUNK : (c + 1) * CHUNK].astype(BF16), upper) + base
        docs.append(part)
        base = part[:, CHUNK - 1 : CHUNK]
    doc8 = jnp.concatenate(docs, axis=1)
    same = [1.0 - starts8]
    for back in range(1, taps - 1):
        moved = pltpu.roll(same[0], back, axis=1)
        same.append(same[-1] * jnp.where(lane < back, 1.0, moved))
    sub = lax.broadcasted_iota(jnp.int32, (8, rows), 0)
    extra = jnp.where(sub == 0, doc8, 0.0)
    for n, m in enumerate(same):
        extra = jnp.where(sub == n + 1, m, extra)
    idx = jnp.broadcast_to(idx_ref[...], (table_rows, rows))
    feat[0:table_rows, :] = (idx == lax.broadcasted_iota(jnp.int32, (table_rows, rows), 0)).astype(F32)
    feat[table_rows : table_rows + 8, :] = extra
    coef[...] = jnp.zeros_like(coef)
    coef[0:table_rows, 0:levels] = table_ref[...]
    coef[table_rows : table_rows + 8, :] = (
        lax.broadcasted_iota(jnp.int32, (8, 128), 0) + DOC_COL
        == lax.broadcasted_iota(jnp.int32, (8, 128), 1)
    ).astype(F32)
    for c in range(chunks):
        aux_ref[c * CHUNK : (c + 1) * CHUNK, :] = dot(
            feat[:, c * CHUNK : (c + 1) * CHUNK], coef[...], ((0,), (0,)), highest
        )

    ends = []
    for c in range(chunks):
        low = c * CHUNK
        masks = [
            jnp.broadcast_to(aux_ref[low : low + CHUNK, DOC_COL + n : DOC_COL + n + 1], (CHUNK, 128))
            for n in range(1, taps)
        ]
        for j in range(0, width, 128):
            total = xs[8 + low : 8 + low + CHUNK, j : j + 128] * cw_ref[0:1, j : j + 128]
            for n in range(1, taps):
                total = total + (
                    xs[8 + low - n : 8 + low - n + CHUNK, j : j + 128] * cw_ref[n : n + 1, j : j + 128]
                ) * masks[n - 1]
            conv_ref[low : low + CHUNK, j : j + 128] = total.astype(BF16)
        ends.append(aux_ref[low + CHUNK - 1 : low + CHUNK, DOC_COL : DOC_COL + 1])
    copy_k.wait()
    copy_v.wait()
    for c in range(chunks):
        low = c * CHUNK
        tail = (aux_ref[low : low + CHUNK, DOC_COL : DOC_COL + 1] == ends[c]).astype(F32)
        tail = jnp.broadcast_to(tail, (CHUNK, 2 * HEAD_DIM))
        conv = conv_ref[low : low + CHUNK, :]
        for h in range(0, HEADS, 2):
            cols = slice(h * HEAD_DIM, (h + 2) * HEAD_DIM)
            key = dot(conv, wk_ref[:, cols])
            value = dot(conv, wv_ref[:, cols]).astype(BF16)
            k_ref[low : low + CHUNK, cols] = key.astype(BF16)
            v_ref[low : low + CHUNK, cols] = value
            kept = (key * tail).astype(BF16)
            for g in range(2):
                lanes = slice(g * HEAD_DIM, (g + 1) * HEAD_DIM)
                st[c, (h + g) * HEAD_DIM : (h + g + 1) * HEAD_DIM, :] = dot(
                    kept[:, lanes], value[:, lanes], ((0,), (0,))
                )

    nodes = [(st[c], ends[c], c) for c in range(chunks)]
    slot = 0
    while len(nodes) > 1:
        merged = []
        for n in range(0, len(nodes), 2):
            left, left_end, _ = nodes[n]
            right, right_end, last = nodes[n + 1]
            loc_ref[slot] = left.astype(BF16)
            slot += 1
            keep = (left_end == right_end).astype(F32)
            merged.append((right + keep * left, right_end, last))
        nodes = merged
    total = nodes[0][0].astype(BF16)
    closed = jnp.broadcast_to((ends[-1] > 0).astype(F32), (FLAG_ROWS, HEAD_DIM)).astype(BF16)
    for n in range(2):
        pay_ref[n, 0:half, :] = total[n * half : (n + 1) * half]
        pay_ref[n, half : half + FLAG_ROWS, :] = closed


def near_kernel(conv_ref, wq_ref, k_ref, v_ref, aux_ref, loc_ref, doc_ref, q_ref, near_ref, weight):
    rows = conv_ref.shape[0]
    chunks = rows // CHUNK
    bits = CHUNK.bit_length() - 1

    @pl.when(pl.program_id(0) == 0)
    def _():
        t = lax.broadcasted_iota(jnp.int32, (CHUNK, CHUNK), 0)
        s = lax.broadcasted_iota(jnp.int32, (CHUNK, CHUNK), 1)
        gap = jnp.bitwise_xor(t, s)
        for c in range(chunks):
            low = c * CHUNK
            lam = aux_ref[low : low + CHUNK, :]
            w = jnp.broadcast_to(lam[:, 0:1], (CHUNK, CHUNK))
            for level in range(1, bits + 1):
                w = jnp.where(gap >= 1 << (level - 1), lam[:, level : level + 1], w)
            same = (lam[:, DOC_COL : DOC_COL + 1] == doc_ref[0:1, low : low + CHUNK]) & (t >= s)
            weight[c] = jnp.where(same, w, 0.0)

    query = dot(conv_ref[...], wq_ref[...]).astype(BF16)
    q_ref[...] = query
    for c in range(chunks):
        low = c * CHUNK
        lam = aux_ref[low : low + CHUNK, :]
        doc = lam[:, DOC_COL : DOC_COL + 1]
        gates = []
        slot, count, level = 0, chunks, bits + 1
        while count > 1:
            node = c * count // chunks
            if node % 2 == 1:
                last = node * (chunks // count) * CHUNK - 1
                end = aux_ref[last : last + 1, DOC_COL : DOC_COL + 1]
                gate = jnp.where(doc == end, lam[:, level : level + 1], 0.0)
                gates.append((slot + node // 2, jnp.broadcast_to(gate, (CHUNK, HEAD_DIM))))
            slot += count // 2
            count //= 2
            level += 1
        for g in range(2):
            lanes = slice(g * HEAD_DIM, (g + 1) * HEAD_DIM)
            q = query[low : low + CHUNK, lanes]
            scores = dot(q, k_ref[low : low + CHUNK, lanes], ((1,), (1,)))
            weighted = (scores * weight[c]).astype(BF16)
            total = dot(weighted, v_ref[low : low + CHUNK, lanes])
            for n, gate in gates:
                total = total + gate * dot(q, loc_ref[n, g * HEAD_DIM : (g + 1) * HEAD_DIM, :])
            near_ref[low : low + CHUNK, lanes] = total


def far_kernel(first_level, q_ref, near_ref, aux_ref, gain_ref, *refs):
    states, out_ref = refs[:-1], refs[-1]
    rows = q_ref.shape[0]
    for low in range(0, rows, CHUNK):
        lam = aux_ref[low : low + CHUNK, :]
        gate = (lam[:, DOC_COL : DOC_COL + 1] == 0.0).astype(F32)
        scales = [
            jnp.broadcast_to(lam[:, first_level + n : first_level + n + 1] * gate, (CHUNK, HEAD_DIM))
            for n in range(len(states))
        ]
        for g in range(2):
            lanes = slice(g * HEAD_DIM, (g + 1) * HEAD_DIM)
            q = q_ref[low : low + CHUNK, lanes]
            total = near_ref[low : low + CHUNK, lanes]
            for scale, state in zip(scales, states):
                total = total + scale * dot(q, state[0, g * HEAD_DIM : (g + 1) * HEAD_DIM, :])
            mean = jnp.mean(total * total, axis=-1, keepdims=True)
            total = total * lax.rsqrt(mean + epsilon) * gain_ref[0:1, lanes]
            out_ref[low : low + CHUNK, lanes] = total.astype(BF16)


def crossed(block, mask):
    size = lax.axis_size("seq")
    return lax.ppermute(block, "seq", [(i, i ^ mask) for i in range(size)])


def joined(own, other, is_right):
    right = jnp.where(is_right, own, other).astype(F32)
    left = jnp.where(is_right, other, own).astype(F32)
    index = (0,) * (own.ndim - 2)
    keep = 1.0 - right[index + (right.shape[-2] - 1, 0)]
    return (right + keep * left).astype(BF16)


def flag_of(block):
    return block[(0,) * (block.ndim - 2) + (block.shape[-2] - 1, 0)].astype(F32)


def shards(
    tokens,
    doc_start,
    level_index,
    level_table,
    conv_weight,
    query_weight,
    key_weight,
    value_weight,
    norm_gain,
):
    rows, width = tokens.shape
    taps = conv_weight.shape[0]
    chunks = rows // CHUNK
    local_bits = rows.bit_length() - 1
    half = HEADS // 2 * HEAD_DIM
    size = lax.axis_size("seq")
    me = lax.axis_index("seq")
    steps = size.bit_length() - 1
    VMEM = pl.BlockSpec(memory_space=pltpu.VMEM)
    ANY = pl.BlockSpec(memory_space=pl.ANY)

    tail = doc_start[rows - 8 :]
    later = jnp.arange(8)[:, None] < jnp.arange(8)[None, :]
    keep = (jnp.sum(jnp.where(later, tail[None, :], 0), axis=1) == 0).astype(tokens.dtype)
    rim = tokens[rows - 8 :] * keep[:, None]
    halo = lax.ppermute(rim, "seq", [(i, i + 1) for i in range(size - 1)])

    starts = doc_start.reshape(1, rows)
    conv, key_rows, values, aux, payload, local_states = pl.pallas_call(
        state_kernel,
        out_shape=(
            jax.ShapeDtypeStruct((rows, width), BF16),
            jax.ShapeDtypeStruct((rows, width), BF16),
            jax.ShapeDtypeStruct((rows, width), BF16),
            jax.ShapeDtypeStruct((rows, 128), F32),
            jax.ShapeDtypeStruct((2, half + FLAG_ROWS, HEAD_DIM), BF16),
            jax.ShapeDtypeStruct((chunks - 1, HEADS * HEAD_DIM, HEAD_DIM), BF16),
        ),
        in_specs=[VMEM] * 6 + [ANY] * 2,
        out_specs=(VMEM,) * 6,
        scratch_shapes=[
            pltpu.VMEM((width, width), BF16),
            pltpu.VMEM((width, width), BF16),
            pltpu.VMEM((rows + 8, width), F32),
            pltpu.VMEM((level_table.shape[0] + 8, rows), F32),
            pltpu.VMEM((level_table.shape[0] + 8, 128), F32),
            pltpu.VMEM((chunks, HEADS * HEAD_DIM, HEAD_DIM), F32),
            pltpu.SemaphoreType.DMA((2,)),
        ],
        compiler_params=pltpu.CompilerParams(vmem_limit_bytes=48 << 20),
        cost_estimate=pl.CostEstimate(
            flops=4 * rows * width * width, bytes_accessed=8 * width * width, transcendentals=0
        ),
        name="conv_key_value_state",
    )(
        tokens,
        halo,
        starts,
        level_index.reshape(1, rows),
        level_table,
        conv_weight,
        key_weight,
        value_weight,
    )

    core = me % 2
    other = crossed(payload, 1)
    is_right = core == 1
    before = jnp.float32(1.0)
    level_states = [(other.astype(F32) * jnp.where(is_right, 1.0, 0.0)).astype(BF16)]
    both = joined(payload, other, is_right)
    before = before * jnp.where(is_right, 1.0 - flag_of(other), 1.0)
    agg = jnp.where(is_right, both[1], both[0])
    for bit in range(1, steps):
        last = bit == steps - 1
        mask = 1 << bit
        if last and bit >= 2:
            mask |= 1 << (bit - 1)
        other = crossed(agg, mask)
        is_right = (me >> bit) % 2 == 1
        mate = crossed(other, 1)
        gate = before * jnp.where(is_right, 1.0, 0.0)
        pair = jnp.where(core == 1, jnp.stack([mate, other]), jnp.stack([other, mate]))
        level_states.append((pair.astype(F32) * gate).astype(BF16))
        before = before * jnp.where(is_right, 1.0 - flag_of(other), 1.0)
        if not last:
            agg = joined(agg, other, is_right)

    docs = jnp.cumsum(doc_start).astype(F32).reshape(1, rows)
    pairs = HEADS // 2
    wide = 2 * HEAD_DIM
    column = pl.BlockSpec((rows, wide), lambda i: (0, i))
    query, near = pl.pallas_call(
        near_kernel,
        grid=(pairs,),
        out_shape=(
            jax.ShapeDtypeStruct((rows, width), BF16),
            jax.ShapeDtypeStruct((rows, width), F32),
        ),
        in_specs=[
            pl.BlockSpec((rows, width), lambda i: (0, 0)),
            column,
            column,
            column,
            pl.BlockSpec((rows, 128), lambda i: (0, 0)),
            pl.BlockSpec((chunks - 1, wide, HEAD_DIM), lambda i: (0, i, 0)),
            pl.BlockSpec((1, rows), lambda i: (0, 0)),
        ],
        out_specs=(column, column),
        scratch_shapes=[pltpu.VMEM((chunks, CHUNK, CHUNK), F32)],
        compiler_params=pltpu.CompilerParams(vmem_limit_bytes=40 << 20),
        cost_estimate=pl.CostEstimate(
            flops=4 * rows * width * width, bytes_accessed=8 * width * width, transcendentals=0
        ),
        name="query_near",
    )(conv, query_weight, key_rows, values, aux, local_states, docs)

    state_spec = pl.BlockSpec((1, wide, HEAD_DIM), lambda i: (i // 2, i % 2, 0))
    return pl.pallas_call(
        functools.partial(far_kernel, local_bits + 1),
        grid=(pairs,),
        out_shape=jax.ShapeDtypeStruct((rows, width), BF16),
        in_specs=[
            column,
            column,
            pl.BlockSpec((rows, 128), lambda i: (0, 0)),
            pl.BlockSpec((1, wide), lambda i: (0, i)),
        ]
        + [state_spec] * steps,
        out_specs=column,
        compiler_params=pltpu.CompilerParams(vmem_limit_bytes=40 << 20),
        cost_estimate=pl.CostEstimate(
            flops=2 * rows * width * width, bytes_accessed=8 * width * width, transcendentals=0
        ),
        name="far_norm",
    )(query, near, aux, norm_gain.reshape(1, width), *level_states)


def solution(mesh):
    split = P(("groups", "seq"))
    in_specs = (P(("groups", "seq"), None), split, split, P(), P(), P(), P(), P(), P())
    return jax.shard_map(
        shards, mesh=mesh, in_specs=in_specs, out_specs=P(("groups", "seq"), None), check_vma=False
    )
```

```python
import functools

import jax
import jax.numpy as jnp
from jax import lax
from jax.experimental import pallas as pl
from jax.experimental.pallas import tpu as pltpu
from jax.sharding import PartitionSpec as P

HEADS = 8
HEAD_DIM = 128
CHUNK = 256
RIM = 16
FLAG_ROWS = 16
DOC_COL = 32
PAIR = 2 * HEAD_DIM
highest = lax.Precision.HIGHEST
epsilon = 1e-05
F32 = jnp.float32
BF16 = jnp.bfloat16
VMEM = pl.BlockSpec(memory_space=pltpu.VMEM)
HBM = pl.BlockSpec(memory_space=pltpu.HBM)
NT = ((1,), (1,))
NN = ((1,), (0,))


def dot(a, b, dims=NN, precision=None):
    return lax.dot_general(a, b, (dims, ((), ())), precision=precision, preferred_element_type=F32)


def iota(shape, axis):
    return lax.broadcasted_iota(jnp.int32, shape, axis)


def rim_kernel(x_hbm, ds_hbm, rim_ref, rows_ref, ds_ref, sems):
    rows = x_hbm.shape[0]
    copies = [
        pltpu.make_async_copy(x_hbm.at[rows - RIM : rows, :], rows_ref, sems.at[0]),
        pltpu.make_async_copy(ds_hbm.at[:, rows - 128 : rows], ds_ref, sems.at[1]),
    ]
    for copy in copies:
        copy.start()
    for copy in copies:
        copy.wait()
    starts = jnp.broadcast_to(ds_ref[...].astype(F32), (RIM, 128))
    later = iota((RIM, 128), 1) > iota((RIM, 128), 0) + (128 - RIM)
    cuts = jnp.sum(jnp.where(later, starts, 0.0), axis=1, keepdims=True)
    rim_ref[...] = jnp.where(cuts == 0.0, rows_ref[...].astype(F32), 0.0).astype(BF16)


def project(c, h, conv, wk_ref, wv_ref, k_out, v_out, tail, eye, st_ref):
    cols = slice(h * HEAD_DIM, h * HEAD_DIM + PAIR)
    key = dot(conv, wk_ref[:, cols]).astype(BF16)
    value = dot(conv, wv_ref[:, cols]).astype(BF16)
    k_out[:, cols] = key
    v_out[:, cols] = value
    turned = (dot(eye, key, NT) * tail).astype(BF16)
    for g in range(2):
        lanes = slice(g * HEAD_DIM, (g + 1) * HEAD_DIM)
        st_ref[(h + g) * HEAD_DIM : (h + g + 1) * HEAD_DIM, :] = dot(turned[lanes, :], value[:, lanes])


def identity():
    return (iota((PAIR, PAIR), 0) == iota((PAIR, PAIR), 1)).astype(BF16)


def body_kernel(
    x_hbm, ds_hbm, cw_hbm, wk_hbm, wv_hbm, wq_hbm,
    head_ref, mask_ref, c0_ref, conv_ref, k_ref, v_ref, st_ref, doc_ref, cw_ref, wk_ref, wv_ref, wq_ref,
    x_ref, xs, col_ref, ds_ref, sems,
):
    rows, width = x_ref.shape
    chunks = rows // CHUNK
    taps = cw_hbm.shape[0]
    order = list(range(1, chunks)) + [0]
    small = [
        pltpu.make_async_copy(ds_hbm, ds_ref, sems.at[0]),
        pltpu.make_async_copy(cw_hbm, cw_ref, sems.at[1]),
    ]
    loads = {
        c: pltpu.make_async_copy(
            x_hbm.at[c * CHUNK : (c + 1) * CHUNK, :], x_ref.at[c * CHUNK : (c + 1) * CHUNK, :], sems.at[2 + c]
        )
        for c in range(chunks)
    }
    weights = [
        pltpu.make_async_copy(source, target, sems.at[2 + chunks + n])
        for n, (source, target) in enumerate(((wk_hbm, wk_ref), (wv_hbm, wv_ref), (wq_hbm, wq_ref)))
    ]
    for copy in small:
        copy.start()
    loads[0].start()
    loads[1].start()
    weights[0].start()
    weights[1].start()
    for c in order[1:-1]:
        loads[c].start()
    weights[2].start()
    for copy in small:
        copy.wait()

    starts = jnp.broadcast_to(ds_ref[...].astype(F32), (8, rows))
    lane = iota((8, rows), 1)
    sub = iota((8, rows), 0)
    same = [1.0 - starts]
    for back in range(1, taps - 1):
        same.append(same[-1] * jnp.where(lane < back, 1.0, pltpu.roll(same[0], back, axis=1)))
    packed = jnp.zeros((8, rows), F32)
    for n, m in enumerate(same):
        packed = jnp.where(sub == n, m, packed)
    for c in range(chunks):
        col_ref[c * CHUNK : (c + 1) * CHUNK, 0:8] = packed[:, c * CHUNK : (c + 1) * CHUNK].T
    mask_ref[:, 0:8] = col_ref[0:RIM, 0:8]

    def widen(c):
        xs[c * CHUNK : (c + 1) * CHUNK, :] = x_ref[c * CHUNK : (c + 1) * CHUNK, :].astype(F32)

    def conv_piece(low, count, cols, out, out_low):
        total = xs[low : low + count, cols] * cw_ref[0:1, cols]
        for n in range(1, taps):
            mask = jnp.broadcast_to(col_ref[low : low + count, n - 1 : n], (count, PAIR))
            total = total + (xs[low - n : low - n + count, cols] * cw_ref[n : n + 1, cols]) * mask
        out[out_low : out_low + count, cols] = total.astype(BF16)

    loads[0].wait()
    widen(0)
    head_ref[...] = xs[0:RIM, :]
    loads[1].wait()
    widen(1)
    for h in range(0, HEADS, 2):
        cols = slice(h * HEAD_DIM, h * HEAD_DIM + PAIR)
        conv_piece(CHUNK, CHUNK, cols, conv_ref, 0)
    upper = (iota((CHUNK, CHUNK), 0) <= iota((CHUNK, CHUNK), 1)).astype(BF16)
    base = jnp.zeros((8, 1), F32)
    for c in range(chunks):
        part = dot(starts[:, c * CHUNK : (c + 1) * CHUNK].astype(BF16), upper) + base
        doc_ref[:, c * CHUNK : (c + 1) * CHUNK] = part
        base = part[:, CHUNK - 1 : CHUNK]
    eye = identity()
    weights[0].wait()
    weights[1].wait()
    for n, c in enumerate(order[:-1]):
        low = c * CHUNK
        here = slice(low - CHUNK, low)
        after = order[n + 1]
        if after != 0:
            loads[after].wait()
            widen(after)
        tail = (doc_ref[0:1, low : low + CHUNK] == doc_ref[0:1, low + CHUNK - 1 : low + CHUNK]).astype(F32)
        conv = conv_ref[here, :]
        for h in range(0, HEADS, 2):
            cols = slice(h * HEAD_DIM, h * HEAD_DIM + PAIR)
            if after == 0:
                conv_piece(RIM, CHUNK - RIM, cols, c0_ref, RIM)
            else:
                conv_piece(after * CHUNK, CHUNK, cols, conv_ref, (after - 1) * CHUNK)
            project(c, h, conv, wk_ref, wv_ref, k_ref.at[here, :], v_ref.at[here, :], tail, eye, st_ref.at[c - 1])
    weights[2].wait()


def first_kernel(
    halo_ref, head_ref, mask_ref, c0_ref, st_ref, doc_ref, cw_ref, wk_ref, wv_ref,
    conv_ref, k_ref, v_ref, pay_ref, loc_ref,
    xs, st0,
):
    taps = cw_ref.shape[0]
    chunks = st_ref.shape[0] + 1
    half = HEADS // 2 * HEAD_DIM
    xs[0:RIM, :] = halo_ref[...].astype(F32)
    xs[RIM : 2 * RIM, :] = head_ref[...]
    total = xs[RIM : 2 * RIM, :] * cw_ref[0:1, :]
    for n in range(1, taps):
        total = total + (xs[RIM - n : 2 * RIM - n, :] * cw_ref[n : n + 1, :]) * mask_ref[:, n - 1 : n]
    conv_ref[0:RIM, :] = total.astype(BF16)
    conv_ref[RIM:CHUNK, :] = c0_ref[RIM:CHUNK, :]
    eye = identity()
    tail = (doc_ref[0:1, 0:CHUNK] == doc_ref[0:1, CHUNK - 1 : CHUNK]).astype(F32)
    conv = conv_ref[...]
    for h in range(0, HEADS, 2):
        project(0, h, conv, wk_ref, wv_ref, k_ref, v_ref, tail, eye, st0)

    def end(c):
        return doc_ref[0:1, (c + 1) * CHUNK - 1 : (c + 1) * CHUNK]

    for h in range(HEADS):
        span = slice(h * HEAD_DIM, (h + 1) * HEAD_DIM)
        nodes = [(st0[span, :], 0)] + [(st_ref[c - 1, span, :], c) for c in range(1, chunks)]
        slot = 0
        while len(nodes) > 1:
            merged = []
            for n in range(0, len(nodes), 2):
                (left, left_last), (right, right_last) = nodes[n], nodes[n + 1]
                loc_ref[slot, span, :] = left.astype(BF16)
                slot += 1
                keep = (end(left_last) == end(right_last)).astype(F32)
                merged.append((right + keep * left, right_last))
            nodes = merged
        low = h * HEAD_DIM % half
        pay_ref[h * HEAD_DIM // half, low : low + HEAD_DIM, :] = nodes[0][0].astype(BF16)
    closed = (end(chunks - 1) > 0).astype(F32)
    for n in range(2):
        pay_ref[n, half : half + FLAG_ROWS, :] = jnp.broadcast_to(closed, (FLAG_ROWS, HEAD_DIM)).astype(BF16)


def fill_aux(idx_hbm, table_hbm, doc_ref, aux_ref, weight_ref, flat_ref, idx_ref, table_ref, sems):
    rows = aux_ref.shape[0]
    chunks = rows // CHUNK
    bits = CHUNK.bit_length() - 1
    levels, table_rows = table_hbm.shape
    copies = [
        pltpu.make_async_copy(idx_hbm, idx_ref, sems.at[0]),
        pltpu.make_async_copy(table_hbm, table_ref, sems.at[1]),
    ]
    for copy in copies:
        copy.start()
    flat_ref[DOC_COL : DOC_COL + 8, :] = doc_ref[...]
    for copy in copies:
        copy.wait()
    idx = jnp.broadcast_to(idx_ref[...], (table_rows, rows))
    onehot = (idx == iota((table_rows, rows), 0)).astype(F32)
    flat_ref[0:levels, :] = dot(table_ref[...], onehot, NN, highest)
    t = iota((CHUNK, CHUNK), 0)
    s = iota((CHUNK, CHUNK), 1)
    gap = jnp.bitwise_xor(t, s)
    for c in range(chunks):
        span = slice(c * CHUNK, (c + 1) * CHUNK)
        lam = flat_ref[:, span].T
        aux_ref[span, :] = lam
        w = jnp.broadcast_to(lam[:, 0:1], (CHUNK, CHUNK))
        for level in range(1, bits + 1):
            w = jnp.where(gap >= 1 << (level - 1), lam[:, level : level + 1], w)
        same = (lam[:, DOC_COL : DOC_COL + 1] == doc_ref[0:1, span]) & (t >= s)
        weight_ref[c] = jnp.where(same, w, 0.0)


def near_heads(pairs, convs, keys, values, wq_ref, aux_ref, weight_ref, loc_ref, q_ref, near_ref):
    rows = aux_ref.shape[0]
    chunks = rows // CHUNK
    bits = CHUNK.bit_length() - 1

    def part(refs, c, cols):
        if c == 0:
            return refs[0][:, cols]
        return refs[1][(c - 1) * CHUNK : c * CHUNK, cols]

    for c in range(chunks):
        span = slice(c * CHUNK, (c + 1) * CHUNK)
        lam = aux_ref[span, :]
        doc = lam[:, DOC_COL : DOC_COL + 1]
        gates = []
        slot, count, level = 0, chunks, bits + 1
        while count > 1:
            node = c * count // chunks
            if node % 2 == 1:
                last = node * (chunks // count) * CHUNK - 1
                end = aux_ref[last : last + 1, DOC_COL : DOC_COL + 1]
                gate = jnp.where(doc == end, lam[:, level : level + 1], 0.0)
                gates.append((slot + node // 2, jnp.broadcast_to(gate, (CHUNK, HEAD_DIM))))
            slot += count // 2
            count //= 2
            level += 1
        conv = part(convs, c, slice(None))
        for m, pair in enumerate(pairs):
            cols = slice(pair * PAIR, (pair + 1) * PAIR)
            query = dot(conv, wq_ref[:, cols]).astype(BF16)
            q_ref[span, m * PAIR : (m + 1) * PAIR] = query
            key, value = part(keys, c, cols), part(values, c, cols)
            for g in range(2):
                lanes = slice(g * HEAD_DIM, (g + 1) * HEAD_DIM)
                state = slice(pair * PAIR + g * HEAD_DIM, pair * PAIR + (g + 1) * HEAD_DIM)
                q = query[:, lanes]
                weighted = (dot(q, key[:, lanes], NT) * weight_ref[c]).astype(BF16)
                total = dot(weighted, value[:, lanes])
                if len(gates) == 2:
                    states = jnp.concatenate([loc_ref[n, state, :] for n, _ in gates], axis=1)
                    product = dot(q, states)
                    total = total + gates[0][1] * product[:, :HEAD_DIM] + gates[1][1] * product[:, HEAD_DIM:]
                else:
                    for n, gate in gates:
                        total = total + gate * dot(q, loc_ref[n, state, :])
                near_ref[span, m * PAIR + g * HEAD_DIM : m * PAIR + (g + 1) * HEAD_DIM] = total


def near_first_kernel(
    pairs, idx_hbm, table_hbm, doc_ref, c0, c1, k0, k1, v0, v1, wq_ref, loc_ref,
    q_ref, near_ref, aux_ref, weight_ref,
    flat_ref, idx_ref, table_ref, sems,
):
    fill_aux(idx_hbm, table_hbm, doc_ref, aux_ref, weight_ref, flat_ref, idx_ref, table_ref, sems)
    near_heads(pairs, (c0, c1), (k0, k1), (v0, v1), wq_ref, aux_ref, weight_ref, loc_ref, q_ref, near_ref)


def near_next_kernel(pairs, c0, c1, k0, k1, v0, v1, wq_ref, loc_ref, aux_ref, weight_ref, q_ref, near_ref):
    near_heads(pairs, (c0, c1), (k0, k1), (v0, v1), wq_ref, aux_ref, weight_ref, loc_ref, q_ref, near_ref)


def joined(own, other, is_right):
    own, other = own.astype(F32), other.astype(F32)
    right = jnp.where(is_right, own, other)
    left = jnp.where(is_right, other, own)
    keep = 1.0 - right[right.shape[0] - 1 :, :]
    return right + keep * left


def join_first_kernel(own_ref, other_ref, out_ref):
    core = lax.axis_index("seq") % 2
    own = jnp.where(core == 1, own_ref[1], own_ref[0])
    other = jnp.where(core == 1, other_ref[1], other_ref[0])
    out_ref[...] = joined(own, other, core == 1).astype(BF16)


def join_kernel(bit, own_ref, other_ref, out_ref):
    out_ref[...] = joined(own_ref[...], other_ref[...], (lax.axis_index("seq") >> bit) % 2 == 1).astype(BF16)


def far_kernel(first_level, steps, q_a, near_a, q_b, near_b, aux_ref, gain_hbm, *refs):
    whole, parts = refs[0], refs[1 : 2 * steps - 1]
    out_hbm, out_ref, gain_ref, sems = refs[2 * steps - 1 :]
    rows, width = out_ref.shape
    half = width // 2
    chunks = rows // CHUNK
    copy = pltpu.make_async_copy(gain_hbm, gain_ref, sems.at[chunks])
    copy.start()
    me = lax.axis_index("seq")
    core = me % 2
    before = jnp.ones((1, HEAD_DIM), F32)
    marks = []
    for n in range(steps):
        bit = jnp.broadcast_to(((me >> n) % 2).astype(F32), (1, HEAD_DIM))
        flag = (whole[0] if n == 0 else parts[2 * n - 2][...])[half : half + 1, :].astype(F32)
        marks.append(bit * before)
        before = before * (1.0 - bit * flag)
    copy.wait()
    stores = []
    for c in range(chunks):
        span = slice(c * CHUNK, (c + 1) * CHUNK)
        lam = aux_ref[span, :]
        gate = (lam[:, DOC_COL : DOC_COL + 1] == 0.0).astype(F32)
        scales = [
            jnp.broadcast_to(lam[:, first_level + n : first_level + n + 1] * gate, (CHUNK, HEAD_DIM)) * marks[n]
            for n in range(steps)
        ]
        for h in range(HEADS):
            q_ref, near_ref = ((q_a, near_a), (q_b, near_b))[h * HEAD_DIM // half]
            low = h * HEAD_DIM % half
            lanes = slice(low, low + HEAD_DIM)
            states = [whole[h * HEAD_DIM // half, lanes, :]]
            for n in range(1, steps):
                mine, mate = parts[2 * n - 2], parts[2 * n - 1]
                low_half = h * HEAD_DIM < half
                states.append(jnp.where((core == 0) == low_half, mine[lanes, :], mate[lanes, :]))
            q = q_ref[span, lanes]
            total = near_ref[span, lanes]
            for n in range(0, steps, 2):
                group = states[n : n + 2]
                product = dot(q, jnp.concatenate(group, axis=1) if len(group) > 1 else group[0])
                for m in range(len(group)):
                    total = total + scales[n + m] * product[:, m * HEAD_DIM : (m + 1) * HEAD_DIM]
            mean = jnp.mean(total * total, axis=-1, keepdims=True)
            cols = slice(h * HEAD_DIM, (h + 1) * HEAD_DIM)
            out_ref[span, cols] = (total * lax.rsqrt(mean + epsilon) * gain_ref[0:1, cols]).astype(BF16)
        store = pltpu.make_async_copy(out_ref.at[span, :], out_hbm.at[span, :], sems.at[c])
        store.start()
        stores.append(store)
    for store in stores:
        store.wait()


def crossed(block, mask):
    size = lax.axis_size("seq")
    return lax.ppermute(block, "seq", [(i, i ^ mask) for i in range(size)])


def pinned(array):
    return pltpu.with_memory_space_constraint(array, pltpu.HBM)


def cost(flops, moved):
    return pl.CostEstimate(flops=flops, bytes_accessed=moved, transcendentals=0)


def params(mib):
    return pltpu.CompilerParams(vmem_limit_bytes=mib << 20)


def shards(
    tokens,
    doc_start,
    level_index,
    level_table,
    conv_weight,
    query_weight,
    key_weight,
    value_weight,
    norm_gain,
):
    rows, width = tokens.shape
    taps = conv_weight.shape[0]
    table_rows, levels = level_table.shape
    chunks = rows // CHUNK
    rest = rows - CHUNK
    local_bits = rows.bit_length() - 1
    half = width // 2
    size = lax.axis_size("seq")
    steps = size.bit_length() - 1
    unit = 2 * rows * width * width
    starts = pinned(doc_start.reshape(1, rows))
    tokens = pinned(tokens)
    shape = jax.ShapeDtypeStruct

    rim = pl.pallas_call(
        rim_kernel,
        out_shape=shape((RIM, width), BF16),
        in_specs=[HBM, HBM],
        out_specs=VMEM,
        scratch_shapes=[
            pltpu.VMEM((RIM, width), BF16),
            pltpu.VMEM((1, 128), jnp.int32),
            pltpu.SemaphoreType.DMA((2,)),
        ],
        compiler_params=params(2),
        name="rim",
    )(tokens, starts)
    halo = lax.ppermute(rim, "seq", [(i, i + 1) for i in range(size - 1)])

    head, mask, c0_part, conv_rest, key_rest, value_rest, states, docs, taps_w, wk, wv, wq = pl.pallas_call(
        body_kernel,
        out_shape=(
            shape((RIM, width), F32),
            shape((RIM, 128), F32),
            shape((CHUNK, width), BF16),
            shape((rest, width), BF16),
            shape((rest, width), BF16),
            shape((rest, width), BF16),
            shape((chunks - 1, HEADS * HEAD_DIM, HEAD_DIM), F32),
            shape((8, rows), F32),
            shape((taps, width), F32),
            shape((width, width), BF16),
            shape((width, width), BF16),
            shape((width, width), BF16),
        ),
        in_specs=[HBM] * 6,
        out_specs=(VMEM,) * 12,
        scratch_shapes=[
            pltpu.VMEM((rows, width), BF16),
            pltpu.VMEM((rows, width), F32),
            pltpu.VMEM((rows, 128), F32),
            pltpu.VMEM((1, rows), jnp.int32),
            pltpu.SemaphoreType.DMA((5 + chunks,)),
        ],
        compiler_params=params(24),
        cost_estimate=cost(2 * unit, 8 * width * width),
        name="body",
    )(tokens, starts, pinned(conv_weight), pinned(key_weight), pinned(value_weight), pinned(query_weight))

    conv0, key0, value0, payload, local_states = pl.pallas_call(
        first_kernel,
        out_shape=(
            shape((CHUNK, width), BF16),
            shape((CHUNK, width), BF16),
            shape((CHUNK, width), BF16),
            shape((2, half + FLAG_ROWS, HEAD_DIM), BF16),
            shape((chunks - 1, HEADS * HEAD_DIM, HEAD_DIM), BF16),
        ),
        in_specs=[VMEM] * 9,
        out_specs=(VMEM,) * 5,
        scratch_shapes=[pltpu.VMEM((2 * RIM, width), F32), pltpu.VMEM((HEADS * HEAD_DIM, HEAD_DIM), F32)],
        compiler_params=params(12),
        cost_estimate=cost(unit, width * width),
        name="first",
    )(halo, head, mask, c0_part, states, docs, taps_w, wk, wv)

    def join(kernel, own, other, name):
        return pl.pallas_call(
            kernel,
            out_shape=shape((half + FLAG_ROWS, HEAD_DIM), BF16),
            in_specs=[VMEM, VMEM],
            out_specs=VMEM,
            compiler_params=params(4),
            cost_estimate=cost(1000, 1000),
            name=name,
        )(own, other)

    other = crossed(payload, 1)
    agg = join(join_first_kernel, payload, other, "join_first")
    far_states = [other]
    for bit in range(1, steps):
        last = bit == steps - 1
        across = 1 << bit
        if last and bit >= 2:
            across |= 1 << (bit - 1)
        other = crossed(agg, across)
        far_states += [other, crossed(other, 1)]
        if not last:
            agg = join(functools.partial(join_kernel, bit), agg, other, "join")

    pairs = HEADS // 2
    shared = (conv0, conv_rest, key0, key_rest, value0, value_rest, wq, local_states)
    query_a, near_a, aux, weight = pl.pallas_call(
        functools.partial(near_first_kernel, tuple(range(pairs // 2))),
        out_shape=(
            shape((rows, half), BF16),
            shape((rows, half), F32),
            shape((rows, 128), F32),
            shape((chunks, CHUNK, CHUNK), F32),
        ),
        in_specs=[HBM, HBM] + [VMEM] * 9,
        out_specs=(VMEM,) * 4,
        scratch_shapes=[
            pltpu.VMEM((128, rows), F32),
            pltpu.VMEM((1, rows), jnp.int32),
            pltpu.VMEM((levels, table_rows), F32),
            pltpu.SemaphoreType.DMA((2,)),
        ],
        compiler_params=params(16),
        cost_estimate=cost(unit, width * width),
        name="near_first",
    )(level_index.reshape(1, rows), level_table.T, docs, *shared)
    query_b, near_b = pl.pallas_call(
        functools.partial(near_next_kernel, tuple(range(pairs // 2, pairs))),
        out_shape=(shape((rows, half), BF16), shape((rows, half), F32)),
        in_specs=[VMEM] * 10,
        out_specs=(VMEM,) * 2,
        compiler_params=params(16),
        cost_estimate=cost(unit, width * width),
        name="near_next",
    )(*shared, aux, weight)

    return pl.pallas_call(
        functools.partial(far_kernel, local_bits + 1, steps),
        out_shape=shape((rows, width), BF16),
        in_specs=[VMEM] * 5 + [HBM] + [VMEM] * (2 * steps - 1),
        out_specs=HBM,
        scratch_shapes=[
            pltpu.VMEM((rows, width), BF16),
            pltpu.VMEM((1, width), F32),
            pltpu.SemaphoreType.DMA((chunks + 1,)),
        ],
        compiler_params=params(26),
        cost_estimate=cost(unit, width * width),
        name="far_norm",
    )(query_a, near_a, query_b, near_b, aux, norm_gain.reshape(1, width), *far_states)


def solution(mesh):
    split = P(("groups", "seq"))
    in_specs = (P(("groups", "seq"), None), split, split, P(), P(), P(), P(), P(), P())
    return jax.shard_map(
        shards, mesh=mesh, in_specs=in_specs, out_specs=P(("groups", "seq"), None), check_vma=False
    )
```
